1024 devices in a mesh: wide: 128 (over x, z, core), lend: 8 (over y).
Axes of the slice: x: 8, y: 8, z: 8, core: 2. Of those that a mesh axis runs over, the one named last changes fastest.
Arguments:
- operators: bfloat16 [8, 128, 1024, 1024], P('lend', 'wide'), as said below
- dual_rhs: float32 [8, 65536, 128], P('lend', 'wide'), may hold values from -6 to 6
- contact: int32 [8, 65536], P('lend', 'wide'), may hold values 0 or 1
- costs: int32 [8, 128], P('lend', 'wide'), may hold values from 1 to 8, as said below
Outputs:
- multipliers: float32 [8, 65536, 128], P('lend', 'wide')
- gradient: float32 [8, 65536, 128], P('lend', 'wide')
The draws below stay inside these ranges and needn't reach their ends.
Inputs may be any that keep to these rules, and one draw needn't show every extreme that they name: `operators`: each subdomain's operator is symmetric positive definite up to rounding. 1 marks a contact multiplier that must stay nonnegative, 0 a gluing one. The number of live blocks of 128 slots of each subdomain; its live slots are the first costs * 128. For every j, costs[2 j, w] + costs[2 j + 1, w] is at most 9.
All inputs are finite; a program needn't handle non-finite values. No bound on the sum of `contact` on one device may be relied on, other than what follows from the above.
Results may differ from the reference program's by a relative error of at most 0.0086.
Values may be sent and summed in bfloat16 or wider, within the bound.
No kernel may reach another device: no remote copies, remote signals or barrier semaphores. Data moves between devices by JAX's collectives and lax.ppermute only.
A program may use at most 32 MiB of HBM per device.

```python
import jax
import jax.numpy as jnp
from jax import lax

M = 1024
ROWBLK = 128
K = 128
ITERS = 4
FACE = 512
MULTS = 65536
N_WIDE = 128
N_LEND = 8


def draw_operators(key, part):

    def single(number):
        subkey = jax.random.fold_in(key, number)
        first_key, second_key = jax.random.split(subkey, 2)
        gaussian = jax.random.normal(first_key, (M, M), jnp.float32)
        coupling = (gaussian + gaussian.T) * (0.5 / jnp.sqrt(2.0 * M))
        diagonal_part = jax.random.uniform(second_key, (M,), jnp.float32, 1.5, 3.0)
        matrix = coupling + jnp.diag(diagonal_part)
        return matrix.astype(jnp.bfloat16)
    stacked = lax.map(single, jnp.arange(N_LEND * N_WIDE, dtype=jnp.int32))
    return stacked.reshape(N_LEND, N_WIDE, M, M)


def draw_costs(key, part):
    most = M // ROWBLK
    base_key = jax.random.fold_in(key, 7301)
    first_key, second_key, third_key = jax.random.split(base_key, 3)
    shape = (N_LEND // 2, N_WIDE)
    heavy = jax.random.randint(first_key, shape, 1, most + 1, dtype=jnp.int32)
    heavy = heavy.at[0, 0].set(most)
    light = jax.random.randint(second_key, shape, 1, most + 2 - heavy, dtype=jnp.int32)
    flip = jax.random.randint(third_key, shape, 0, 2, dtype=jnp.int32)
    flip = flip.at[0, 0].set(0)
    upper = jnp.where(flip == 1, light, heavy)
    lower = jnp.where(flip == 1, heavy, light)
    paired = jnp.stack([upper, lower], axis=1)
    return paired.reshape(N_LEND, N_WIDE).astype(jnp.int32)


def with_ends(values, stream_key, smallest, top_value):
    longest = values.shape.index(max(values.shape))
    spots = []
    for shift in (0, 1):
        where = [jax.random.randint(jax.random.fold_in(stream_key, axis), (), 0, length) for axis, length in enumerate(values.shape)]
        where[longest] = (where[longest] + shift) % values.shape[longest]
        spots.append(tuple(where))
    return values.at[spots[0]].set(smallest).at[spots[1]].set(top_value)


def block_scale(rng, extent, shards, low, largest):
    loudness = 1.0
    for axis_at, parts in shards:
        heights = jax.random.uniform(jax.random.fold_in(jax.random.fold_in(rng, 6), axis_at), (parts,), jnp.float32, low / len(shards), largest / len(shards))
        loudness = loudness * jnp.repeat(jnp.exp(heights), extent[axis_at] // parts).reshape((-1,) + (1,) * (len(extent) - 1 - axis_at))
    return loudness


def noise(key, dims, width, bound, cuts=(), held_as=jnp.bfloat16):
    factor_of = block_scale(key, dims, cuts, -0.22, 0.18) if cuts else 1.0
    entries = jax.random.normal(key, dims, jnp.float32) * width * factor_of
    return jnp.minimum(jnp.maximum(entries, -bound), bound).astype(held_as)


def setup_inputs(seed: int = 0) -> dict:
    streams_of = jax.random.split(jax.random.key(seed), 5)
    operators = draw_operators(jax.random.fold_in(streams_of[4], 71), 0)
    dual_rhs = noise(streams_of[1], (N_LEND, MULTS, K), 1.0, 6.0, ((0, 8), (1, 128)), jnp.float32)
    contact = with_ends((jax.random.randint(streams_of[2], (N_LEND, MULTS), 0, 2) < 1).astype(jnp.int32), jax.random.fold_in(streams_of[2], 1), 0, 1)
    costs = draw_costs(jax.random.fold_in(streams_of[4], 71), 0)
    return {"operators": operators, "dual_rhs": dual_rhs, "contact": contact, "costs": costs}


RIDGE = 1.0
FIRST_STEP = 0.1
EPSILON = 1e-6


def project(values, contact):
    return jnp.where(contact[..., None] == 1, jnp.maximum(values, 0.0), values)


def dual_apply(operators, costs, field):
    blocks = field.reshape(N_LEND, N_WIDE, FACE, K).astype(jnp.bfloat16)
    previous = jnp.roll(blocks, 1, axis=1)
    operand = jnp.concatenate([-previous, blocks], axis=2)
    slots = jnp.arange(M, dtype=jnp.int32)
    active = slots[None, None, :, None] < (costs * ROWBLK)[:, :, None, None]
    operand = jnp.where(active, operand, jnp.zeros_like(operand))

    def single(items):
        matrix, vectors, keep = items
        product = jnp.dot(matrix, vectors, preferred_element_type=jnp.float32)
        return jnp.where(keep, product, jnp.float32(0.0))

    products = lax.map(single, (operators.reshape(N_LEND * N_WIDE, M, M), operand.reshape(N_LEND * N_WIDE, M, K), active.reshape(N_LEND * N_WIDE, M, 1)))
    products = products.reshape(N_LEND, N_WIDE, M, K)
    summed = products[:, :, FACE:, :] - jnp.roll(products[:, :, :FACE, :], -1, axis=1)
    return summed.reshape(N_LEND, MULTS, K) + RIDGE * field


def reference(operators, dual_rhs, contact, costs):
    multipliers = jnp.zeros(dual_rhs.shape, jnp.float32)
    image = jnp.zeros(dual_rhs.shape, jnp.float32)
    gradient = -dual_rhs
    steplen = jnp.full((N_LEND, 1, K), FIRST_STEP, jnp.float32)
    for iteration in range(ITERS):
        moved = project(multipliers - steplen * gradient, contact)
        change = moved - multipliers
        response = dual_apply(operators, costs, change)
        image = image + response
        gradient = image - dual_rhs
        multipliers = moved
        if iteration + 1 < ITERS:
            numer = jnp.sum(change * change, axis=1, keepdims=True)
            denom = jnp.sum(change * response, axis=1, keepdims=True)
            steplen = (numer + EPSILON) / (denom + EPSILON)
    return (multipliers, gradient)
```

```python
import functools

import jax
import jax.numpy as jnp
from jax import lax
from jax.experimental import pallas as pl
from jax.experimental.pallas import tpu as pltpu
from jax.sharding import PartitionSpec as P

ROWBLK = 128
ITERS = 4
RIDGE = 1.0
FIRST_STEP = 0.1
EPSILON = 1e-6
CHUNK = 128
TILE = 256

VMEM = pl.BlockSpec(memory_space=pltpu.VMEM)
SMEM = pl.BlockSpec(memory_space=pltpu.SMEM)


def fold(values):
    return jnp.sum(values.reshape(values.shape[0] // 8, 8, values.shape[1]), axis=0)


def advance(chunk, step, m_ref, g_ref, lo_ref, m_out, sign):
    rows = pl.ds(chunk * CHUNK, CHUNK)
    old = m_ref[rows, :] if m_ref is not None else None
    trial = -(step * g_ref[rows, :]) if old is None else old - step * g_ref[rows, :]
    moved = jnp.maximum(trial, lo_ref[rows, :])
    change = moved if old is None else moved - old
    m_out[rows, :] = moved
    return change


def product(par, live, k_ref, u_ref, c_ref, y_ref):
    face = c_ref.shape[0] // 2
    denom = jnp.zeros((8, c_ref.shape[1]), jnp.float32)
    operand = u_ref[...]
    for half in range(2):
        base = face * ((1 - par) if half == 0 else par)
        sign = jnp.where((par == 0) == (half == 0), 1.0, -1.0)
        total = jnp.zeros_like(denom)
        for t in range(face // TILE):
            off = pl.multiple_of(base + t * TILE, TILE)
            piece = jnp.dot(k_ref[pl.ds(off, TILE), :], operand, preferred_element_type=jnp.float32)
            slots = off + lax.broadcasted_iota(jnp.int32, piece.shape, 0)
            piece = jnp.where(slots < live * ROWBLK, piece, 0.0)
            rows = pl.ds(half * face + t * TILE, TILE)
            y_ref[half][pl.ds(t * TILE, TILE), :] = piece
            total = total + fold(piece * c_ref[rows, :])
        denom = denom + sign * total
    return jnp.sum(denom, axis=0, keepdims=True)


def store_operand(par, live, chunk, change, face, u_ref):
    half = (chunk * CHUNK) // face
    base = face * ((1 - par) if half == 0 else par)
    sign = jnp.where((par == 0) == (half == 0), 1.0, -1.0)
    off = pl.multiple_of(base + chunk * CHUNK - half * face, CHUNK)
    slots = off + lax.broadcasted_iota(jnp.int32, change.shape, 0)
    kept = jnp.where(slots < live * ROWBLK, change * sign, 0.0)
    u_ref[pl.ds(off, CHUNK), :] = kept.astype(jnp.bfloat16)


def partials(par, squares, denom, send_ref):
    own = jnp.where(par == 0, squares[0], squares[1])
    numer = jnp.sum(own, axis=0, keepdims=True)
    both = jnp.concatenate([numer, denom + RIDGE * numer], axis=0)
    send_ref[...] = jnp.broadcast_to(both[None], send_ref.shape)


def first_kernel(par_ref, live_ref, k_ref, own_ref, prev_ref, flag_own_ref, flag_prev_ref,
                 send_ref, near_ref, far_ref, m_ref, g_ref, lo_ref, c_ref, u_ref):
    par = par_ref[0, 0]
    live = live_ref[0, 0]
    face = own_ref.shape[0]
    own_base = face * par
    prev_base = face * (1 - par)
    for rhs, flags, base in ((own_ref, flag_own_ref, own_base), (prev_ref, flag_prev_ref, prev_base)):
        for t in range(face // CHUNK):
            off = pl.multiple_of(base + t * CHUNK, CHUNK)
            row = flags[0:1, t * CHUNK:(t + 1) * CHUNK].astype(jnp.float32)
            column = jnp.broadcast_to(row, (CHUNK, CHUNK)).T
            lo_ref[pl.ds(off, CHUNK), :] = jnp.where(column == 1.0, 0.0, -jnp.inf)
            g_ref[pl.ds(off, CHUNK), :] = -rhs[pl.ds(t * CHUNK, CHUNK), :]
    squares = [jnp.zeros((8, own_ref.shape[1]), jnp.float32) for _ in range(2)]
    for chunk in range(2 * face // CHUNK):
        change = advance(chunk, FIRST_STEP, None, g_ref, lo_ref, m_ref, None)
        c_ref[pl.ds(chunk * CHUNK, CHUNK), :] = change
        half = (chunk * CHUNK) // face
        squares[half] = squares[half] + fold(change * change)
        store_operand(par, live, chunk, change, face, u_ref)
    denom = product(par, live, k_ref, u_ref, c_ref, (near_ref, far_ref))
    partials(par, squares, denom, send_ref)


def step_kernel(last, par_ref, live_ref, k_ref, sums_ref, near_in, far_in, near_got, far_got,
                m_in, g_in, lo_ref, c_in, *outs):
    if last:
        top_ref, pre_ref, own_ref, g_ref, m_ref, c_ref, u_ref, near_ref, far_ref = outs
    else:
        send_ref, near_ref, far_ref, m_ref, g_ref, c_ref, u_ref = outs
    par = par_ref[0, 0]
    live = live_ref[0, 0]
    face = near_in.shape[0]
    total = sums_ref[...]
    count = total.shape[0]
    while count > 1:
        count //= 2
        total = total[:count] + total[count:]
    total = total[0]
    step = (total[0:1, :] + EPSILON) / (total[1:2, :] + EPSILON)
    squares = [jnp.zeros((8, near_in.shape[1]), jnp.float32) for _ in range(2)]
    for chunk in range(2 * face // CHUNK):
        rows = pl.ds(chunk * CHUNK, CHUNK)
        half = (chunk * CHUNK) // face
        inner = pl.ds(chunk * CHUNK - half * face, CHUNK)
        mine, got = ((near_in, near_got), (far_in, far_got))[half]
        sign = jnp.where((par == 0) == (half == 0), 1.0, -1.0)
        response = (mine[inner, :] - got[inner, :]) * sign + RIDGE * c_in[rows, :]
        grad = g_in[rows, :] + response
        g_ref[rows, :] = grad
        old = m_in[rows, :]
        moved = jnp.maximum(old - step * grad, lo_ref[rows, :])
        change = moved - old
        m_ref[rows, :] = moved
        c_ref[rows, :] = change
        if not last:
            squares[half] = squares[half] + fold(change * change)
        store_operand(par, live, chunk, change, face, u_ref)
    denom = product(par, live, k_ref, u_ref, c_ref, (near_ref, far_ref))
    if not last:
        partials(par, squares, denom, send_ref)
        return
    own = pl.ds(pl.multiple_of(face * par, face), face)
    own_ref[...] = m_ref[own, :]
    base = g_ref[own, :] + RIDGE * c_ref[own, :]

    @pl.when(par == 0)
    def _():
        top_ref[...] = far_ref[...]
        pre_ref[...] = base + near_ref[...]

    @pl.when(par != 0)
    def _():
        top_ref[...] = near_ref[...]
        pre_ref[...] = base + far_ref[...]


def on_device(operators, dual_rhs, contact, costs, *, wide):
    matrix = operators[0, 0]
    rhs = dual_rhs[0]
    face, cases = rhs.shape
    order = 2 * face
    par = (lax.axis_index("wide") % 2).astype(jnp.int32).reshape(1, 1)
    forward = [(i, (i + 1) % wide) for i in range(wide)]
    backward = [((i + 1) % wide, i) for i in range(wide)]
    near_pairs = [(i, i ^ 1) for i in range(wide)]
    far_pairs = [(i, ((i + 1) ^ 1) - 1 if i % 2 else (i - 1) % wide) for i in range(wide)]
    far_pairs = [(i, (i + 1) % wide if i % 2 else (i - 1) % wide) for i in range(wide)]

    rhs_prev = lax.ppermute(rhs, "wide", forward)
    flag_prev = lax.ppermute(contact, "wide", forward)

    f32 = jnp.float32
    send_s = jax.ShapeDtypeStruct((wide, 2, cases), f32)
    half_s = jax.ShapeDtypeStruct((face, cases), f32)
    full_s = jax.ShapeDtypeStruct((order, cases), f32)
    params = pltpu.CompilerParams(vmem_limit_bytes=16 << 20)
    cost = pl.CostEstimate(flops=2 * order * order * cases, bytes_accessed=2 * order * order,
                           transcendentals=0)
    operand = pltpu.VMEM((order, cases), jnp.bfloat16)

    send, near, far, m, g, lo, c = pl.pallas_call(
        first_kernel,
        out_shape=(send_s, half_s, half_s, full_s, full_s, full_s, full_s),
        in_specs=[SMEM, SMEM] + [VMEM] * 5,
        out_specs=(VMEM,) * 7,
        scratch_shapes=[operand],
        compiler_params=params,
        cost_estimate=cost,
        name="first",
    )(par, costs, matrix, rhs, rhs_prev, contact, flag_prev)

    for iteration in range(1, ITERS):
        last = iteration + 1 == ITERS
        sums = lax.all_to_all(send, "wide", 0, 0)
        near_got = lax.ppermute(near, "wide", near_pairs)
        far_got = lax.ppermute(far, "wide", far_pairs)
        args = (par, costs, matrix, sums, near, far, near_got, far_got, m, g, lo, c)
        if not last:
            send, near, far, m, g, c = pl.pallas_call(
                functools.partial(step_kernel, False),
                out_shape=(send_s, half_s, half_s, full_s, full_s, full_s),
                in_specs=[SMEM, SMEM] + [VMEM] * 10,
                out_specs=(VMEM,) * 6,
                scratch_shapes=[operand],
                compiler_params=params,
                cost_estimate=cost,
                name="step",
            )(*args)
        else:
            full = pltpu.VMEM((order, cases), f32)
            half = pltpu.VMEM((face, cases), f32)
            top, pre, own = pl.pallas_call(
                functools.partial(step_kernel, True),
                out_shape=(half_s, half_s, half_s),
                in_specs=[SMEM, SMEM] + [VMEM] * 10,
                out_specs=(VMEM,) * 3,
                scratch_shapes=[full, full, full, operand, half, half],
                compiler_params=params,
                cost_estimate=cost,
                name="last",
            )(*args)
    gradient = pre - lax.ppermute(top, "wide", backward)
    return own[None], gradient[None]


def solution(mesh):
    return jax.shard_map(
        functools.partial(on_device, wide=mesh.shape["wide"]),
        mesh=mesh,
        in_specs=(
            P("lend", "wide", None, None),
            P("lend", "wide", None),
            P("lend", "wide"),
            P("lend", "wide"),
        ),
        out_specs=(P("lend", "wide", None), P("lend", "wide", None)),
        check_vma=False,
    )
```

```python
import functools

import jax
import jax.numpy as jnp
from jax import lax
from jax.experimental import pallas as pl
from jax.experimental.pallas import tpu as pltpu
from jax.sharding import Mesh
from jax.sharding import PartitionSpec as P


ROWBLK = 128
ITERS = 4
RIDGE = 1.0
FIRST_STEP = 0.1
EPSILON = 1e-6
CHUNK = 128
TILE = 256
EXTRA = 8
WIDE = ("chip", "core")

HBM = pl.BlockSpec(memory_space=pltpu.HBM)
VMEM = pl.BlockSpec(memory_space=pltpu.VMEM)
SMEM = pl.BlockSpec(memory_space=pltpu.SMEM)


def base_of(par, half, face):
    return face * ((1 - par) if half == 0 else par)


def sign_of(par, half):
    return jnp.where((par == 0) == (half == 0), 1.0, -1.0)


def fold(values):
    return jnp.sum(values.reshape(values.shape[0] // 8, 8, values.shape[1]), axis=0)


def set_face(rhs, flags, base, g_ref, lo_ref):
    for t in range(rhs.shape[0] // CHUNK):
        off = pl.multiple_of(base + t * CHUNK, CHUNK)
        row = flags[0:1, t * CHUNK:(t + 1) * CHUNK].astype(jnp.float32)
        column = jnp.broadcast_to(row, (CHUNK, CHUNK)).T
        lo_ref[pl.ds(off, CHUNK), :] = jnp.where(column == 1.0, 0.0, -jnp.inf).astype(lo_ref.dtype)
        g_ref[pl.ds(off, CHUNK), :] = -rhs[pl.ds(t * CHUNK, CHUNK), :]


def store_operand(par, live, chunk, change, face, u_ref):
    half = (chunk * CHUNK) // face
    off = pl.multiple_of(base_of(par, half, face) + chunk * CHUNK - half * face, CHUNK)
    slots = off + lax.broadcasted_iota(jnp.int32, change.shape, 0)
    kept = jnp.where(slots < live * ROWBLK, change * sign_of(par, half), 0.0)
    u_ref[pl.ds(off, CHUNK), :] = kept.astype(jnp.bfloat16)


def tile_product(off, live, k_ref, operand):
    off = pl.multiple_of(off, TILE)
    piece = jnp.dot(k_ref[pl.ds(off, TILE), :], operand, preferred_element_type=jnp.float32)
    slots = off + lax.broadcasted_iota(jnp.int32, piece.shape, 0)
    return jnp.where(slots < live * ROWBLK, piece, 0.0)


def product(par, live, squares, k_ref, u_ref, g_ref, c_ref, q_ref, near_ref, far_ref):
    face = far_ref.shape[0]
    operand = u_ref[...]
    denom = jnp.zeros((8, c_ref.shape[1]), jnp.float32)
    for half in range(2):
        sign = sign_of(par, half)
        total = jnp.zeros_like(denom)
        for t in range(face // TILE):
            piece = tile_product(base_of(par, half, face) + t * TILE, live, k_ref, operand)
            rows = pl.ds(half * face + t * TILE, TILE)
            (near_ref, far_ref)[half][pl.ds(t * TILE, TILE), :] = piece
            change = c_ref[rows, :]
            q_ref[rows, :] = g_ref[rows, :] + RIDGE * change + sign * piece
            total = total + fold(piece * change)
        denom = denom + sign * total
    own = jnp.where(par == 0, squares[0], squares[1])
    numer = jnp.sum(own, axis=0, keepdims=True)
    denom = jnp.sum(denom, axis=0, keepdims=True) + RIDGE * numer
    rest = jnp.zeros((EXTRA - 2, c_ref.shape[1]), jnp.float32)
    near_ref[pl.ds(face, EXTRA), :] = jnp.concatenate([numer, denom, rest], axis=0)


def prep_kernel(k_hbm, rhs_hbm, flag_hbm, g_ref, lo_ref, held_ref, rhs_ref, flag_ref, sems):
    whole = pltpu.make_async_copy(k_hbm, held_ref, sems.at[0])
    rhs = pltpu.make_async_copy(rhs_hbm, rhs_ref, sems.at[1])
    flag = pltpu.make_async_copy(flag_hbm, flag_ref, sems.at[2])
    rhs.start()
    flag.start()
    whole.start()
    rhs.wait()
    flag.wait()
    set_face(rhs_ref, flag_ref, 0, g_ref, lo_ref)
    whole.wait()


def first_kernel(par_ref, live_ref, k_ref, own_g_ref, own_lo_ref, prev_ref, flag_prev_ref,
                 near_ref, far_ref, m_ref, q_ref, lo_ref, g_ref, c_ref, u_ref):
    par = par_ref[0, 0]
    live = live_ref[0, 0]
    face = prev_ref.shape[0]
    own = pl.ds(pl.multiple_of(face * par, face), face)
    g_ref[own, :] = own_g_ref[...]
    lo_ref[own, :] = own_lo_ref[...]
    set_face(prev_ref, flag_prev_ref, face * (1 - par), g_ref, lo_ref)
    squares = [jnp.zeros((8, prev_ref.shape[1]), jnp.float32) for _ in range(2)]
    for chunk in range(2 * face // CHUNK):
        rows = pl.ds(chunk * CHUNK, CHUNK)
        half = (chunk * CHUNK) // face
        change = jnp.maximum(-(FIRST_STEP * g_ref[rows, :]), lo_ref[rows, :].astype(jnp.float32))
        m_ref[rows, :] = change
        c_ref[rows, :] = change
        squares[half] = squares[half] + fold(change * change)
        store_operand(par, live, chunk, change, face, u_ref)
    product(par, live, squares, k_ref, u_ref, g_ref, c_ref, q_ref, near_ref, far_ref)


def pair_kernel(near_ref, got_ref, send_ref):
    rows = pl.ds(near_ref.shape[0] - EXTRA, EXTRA)
    both = near_ref[rows, :] + got_ref[rows, :]
    send_ref[...] = jnp.broadcast_to(both[None, 0:2, :], send_ref.shape)


def total_kernel(sums_ref, step_ref):
    total = sums_ref[...]
    count = total.shape[0]
    while count > 1:
        count //= 2
        total = total[:count] + total[count:]
    total = total[0]
    step_ref[...] = (total[0:1, :] + EPSILON) / (total[1:2, :] + EPSILON)


def step_kernel(last, par_ref, live_ref, k_ref, step_ref, near_got, far_got, m_in, q_in, lo_ref, *outs):
    if last:
        top_ref, base_ref, own_ref, u_ref, g_ref, m_ref, c_ref = outs
    else:
        near_ref, far_ref, m_ref, q_ref, g_ref, c_ref, u_ref = outs
    par = par_ref[0, 0]
    live = live_ref[0, 0]
    face = far_got.shape[0]
    step = step_ref[...]
    squares = [jnp.zeros((8, far_got.shape[1]), jnp.float32) for _ in range(2)]
    for chunk in range(2 * face // CHUNK):
        rows = pl.ds(chunk * CHUNK, CHUNK)
        half = (chunk * CHUNK) // face
        inner = pl.ds(chunk * CHUNK - half * face, CHUNK)
        got = (near_got, far_got)[half]
        grad = q_in[rows, :] - sign_of(par, half) * got[inner, :]
        g_ref[rows, :] = grad
        old = m_in[rows, :]
        moved = jnp.maximum(old - step * grad, lo_ref[rows, :].astype(jnp.float32))
        change = moved - old
        m_ref[rows, :] = moved
        c_ref[rows, :] = change
        if not last:
            squares[half] = squares[half] + fold(change * change)
        store_operand(par, live, chunk, change, face, u_ref)
    if not last:
        product(par, live, squares, k_ref, u_ref, g_ref, c_ref, q_ref, near_ref, far_ref)
        return
    operand = u_ref[...]
    for t in range(face // TILE):
        top_ref[pl.ds(t * TILE, TILE), :] = tile_product(t * TILE, live, k_ref, operand)
    own = pl.ds(pl.multiple_of(face * par, face), face)
    own_ref[...] = m_ref[own, :]
    base_ref[...] = g_ref[own, :] + RIDGE * c_ref[own, :]


def tail_kernel(live_ref, k_ref, u_ref, base_ref, own_ref, pre_ref, out_ref):
    face = base_ref.shape[0]
    operand = u_ref[...]
    out_ref[...] = own_ref[...]
    for t in range(face // TILE):
        rows = pl.ds(t * TILE, TILE)
        pre_ref[rows, :] = base_ref[rows, :] + tile_product(face + t * TILE, live_ref[0, 0], k_ref, operand)


def on_device(operators, dual_rhs, contact, costs, *, chips):
    matrix = pltpu.with_memory_space_constraint(operators[0, 0], pltpu.HBM)
    rhs = dual_rhs[0]
    face, cases = rhs.shape
    order = 2 * face
    wide = 2 * chips
    par = lax.axis_index("core").astype(jnp.int32).reshape(1, 1)
    forward = [(i, (i + 1) % wide) for i in range(wide)]
    backward = [((i + 1) % wide, i) for i in range(wide)]
    near_pairs = [(i, i ^ 1) for i in range(wide)]
    far_pairs = [(i, (i + 1) % wide if i % 2 else (i - 1) % wide) for i in range(wide)]

    rhs_prev = lax.ppermute(rhs, WIDE, forward)
    flag_prev = lax.ppermute(contact, WIDE, forward)

    f32, bf16 = jnp.float32, jnp.bfloat16
    send_s = jax.ShapeDtypeStruct((chips, 2, cases), f32)
    near_s = jax.ShapeDtypeStruct((face + EXTRA, cases), f32)
    half_s = jax.ShapeDtypeStruct((face, cases), f32)
    full_s = jax.ShapeDtypeStruct((order, cases), f32)
    low_s = jax.ShapeDtypeStruct((order, cases), bf16)
    full = pltpu.VMEM((order, cases), f32)
    operand = pltpu.VMEM((order, cases), bf16)
    call = functools.partial(
        pl.pallas_call,
        compiler_params=pltpu.CompilerParams(vmem_limit_bytes=16 << 20),
        cost_estimate=pl.CostEstimate(
            flops=2 * order * order * cases, bytes_accessed=2 * order * order, transcendentals=0
        ),
    )

    own_g, own_lo, held = call(
        prep_kernel,
        out_shape=(
            half_s,
            jax.ShapeDtypeStruct((face, cases), bf16),
            jax.ShapeDtypeStruct(matrix.shape, matrix.dtype),
        ),
        in_specs=[HBM] * 3,
        out_specs=(VMEM,) * 3,
        scratch_shapes=[
            pltpu.VMEM(rhs.shape, f32),
            pltpu.VMEM(contact.shape, contact.dtype),
            pltpu.SemaphoreType.DMA((3,)),
        ],
        name="prep",
    )(
        matrix,
        pltpu.with_memory_space_constraint(rhs, pltpu.HBM),
        pltpu.with_memory_space_constraint(contact, pltpu.HBM),
    )
    near, far, m, q, lo = call(
        first_kernel,
        out_shape=(near_s, half_s, full_s, full_s, low_s),
        in_specs=[SMEM, SMEM] + [VMEM] * 5,
        out_specs=(VMEM,) * 5,
        scratch_shapes=[full, full, operand],
        name="first",
    )(par, costs, held, own_g, own_lo, rhs_prev, flag_prev)

    for iteration in range(1, ITERS):
        last = iteration + 1 == ITERS
        near_got = lax.ppermute(near, WIDE, near_pairs)
        far_got = lax.ppermute(far, WIDE, far_pairs)
        send = call(
            pair_kernel,
            out_shape=send_s,
            in_specs=[VMEM, VMEM],
            out_specs=VMEM,
            name="pair",
        )(near, near_got)
        sums = lax.all_to_all(send, "chip", 0, 0)
        steplen = call(
            total_kernel,
            out_shape=jax.ShapeDtypeStruct((1, cases), f32),
            in_specs=[VMEM],
            out_specs=VMEM,
            name="total",
        )(sums)
        args = (par, costs, held, steplen, near_got, far_got, m, q, lo)
        if not last:
            near, far, m, q = call(
                functools.partial(step_kernel, False),
                out_shape=(near_s, half_s, full_s, full_s),
                in_specs=[SMEM, SMEM] + [VMEM] * 7,
                out_specs=(VMEM,) * 4,
                scratch_shapes=[full, full, operand],
                name="step",
            )(*args)
        else:
            top, base, own, u = call(
                functools.partial(step_kernel, True),
                out_shape=(half_s, half_s, half_s, low_s),
                in_specs=[SMEM, SMEM] + [VMEM] * 7,
                out_specs=(VMEM,) * 4,
                scratch_shapes=[full, full, full],
                name="last",
            )(*args)
    got = lax.ppermute(top, WIDE, backward)
    pre, own = call(
        tail_kernel,
        out_shape=(half_s, half_s),
        in_specs=[SMEM] + [VMEM] * 4,
        out_specs=(VMEM,) * 2,
        name="tail",
    )(costs, held, u, base, own)
    gradient = pre - got
    return own[None], gradient[None]


def solution(mesh):
    chips = mesh.shape["wide"] // 2
    finer = Mesh(mesh.devices.reshape(chips, 2, mesh.shape["lend"]), WIDE + ("lend",))
    return jax.shard_map(
        functools.partial(on_device, chips=chips),
        mesh=finer,
        in_specs=(
            P("lend", WIDE, None, None),
            P("lend", WIDE, None),
            P("lend", WIDE),
            P("lend", WIDE),
        ),
        out_specs=(P("lend", WIDE, None), P("lend", WIDE, None)),
        check_vma=False,
    )
```

```python
import functools

import jax
import jax.numpy as jnp
from jax import lax
from jax.experimental import pallas as pl
from jax.experimental.pallas import tpu as pltpu
from jax.sharding import Mesh
from jax.sharding import PartitionSpec as P


ROWBLK = 128
ITERS = 4
RIDGE = 1.0
FIRST_STEP = 0.1
EPSILON = 1e-6
CHUNK = 128
TILE = 256
EXTRA = 8
WIDE = ("chip", "core")

HBM = pl.BlockSpec(memory_space=pltpu.HBM)
VMEM = pl.BlockSpec(memory_space=pltpu.VMEM)
SMEM = pl.BlockSpec(memory_space=pltpu.SMEM)


def base_of(par, half, face):
    return face * ((1 - par) if half == 0 else par)


def sign_of(par, half):
    return jnp.where((par == 0) == (half == 0), 1.0, -1.0)


def fold(values):
    return jnp.sum(values.reshape(values.shape[0] // 8, 8, values.shape[1]), axis=0)


def set_face(rhs, flags, base, g_ref, lo_ref):
    for t in range(rhs.shape[0] // CHUNK):
        off = pl.multiple_of(base + t * CHUNK, CHUNK)
        row = flags[0:1, t * CHUNK:(t + 1) * CHUNK].astype(jnp.float32)
        column = jnp.broadcast_to(row, (CHUNK, CHUNK)).T
        lo_ref[pl.ds(off, CHUNK), :] = jnp.where(column == 1.0, 0.0, -jnp.inf).astype(lo_ref.dtype)
        g_ref[pl.ds(off, CHUNK), :] = -rhs[pl.ds(t * CHUNK, CHUNK), :]


def store_operand(par, live, chunk, change, face, u_ref):
    half = (chunk * CHUNK) // face
    off = pl.multiple_of(base_of(par, half, face) + chunk * CHUNK - half * face, CHUNK)
    slots = off + lax.broadcasted_iota(jnp.int32, change.shape, 0)
    kept = jnp.where(slots < live * ROWBLK, change * sign_of(par, half), 0.0)
    u_ref[pl.ds(off, CHUNK), :] = kept.astype(jnp.bfloat16)


def tile_product(off, live, k_ref, operand):
    off = pl.multiple_of(off, TILE)
    piece = jnp.dot(k_ref[pl.ds(off, TILE), :], operand, preferred_element_type=jnp.float32)
    slots = off + lax.broadcasted_iota(jnp.int32, piece.shape, 0)
    return jnp.where(slots < live * ROWBLK, piece, 0.0)


def product(par, live, squares, k_ref, u_ref, g_ref, c_ref, q_ref, near_ref, far_ref):
    face = far_ref.shape[0]
    operand = u_ref[...]
    denom = jnp.zeros((8, c_ref.shape[1]), jnp.float32)
    for half in range(2):
        sign = sign_of(par, half)
        total = jnp.zeros_like(denom)
        for t in range(face // TILE):
            piece = tile_product(base_of(par, half, face) + t * TILE, live, k_ref, operand)
            rows = pl.ds(half * face + t * TILE, TILE)
            sent = (near_ref, far_ref)[half]
            sent[pl.ds(t * TILE, TILE), :] = piece.astype(sent.dtype)
            change = c_ref[rows, :]
            q_ref[rows, :] = g_ref[rows, :] + RIDGE * change + sign * piece
            total = total + fold(piece * change)
        denom = denom + sign * total
    own = jnp.where(par == 0, squares[0], squares[1])
    numer = jnp.sum(own, axis=0, keepdims=True)
    denom = jnp.sum(denom, axis=0, keepdims=True) + RIDGE * numer
    rest = jnp.zeros((EXTRA - 2, c_ref.shape[1]), jnp.float32)
    near_ref[pl.ds(face, EXTRA), :] = jnp.concatenate([numer, denom, rest], axis=0)


def prep_kernel(k_hbm, rhs_hbm, flag_hbm, g_ref, lo_ref, held_ref, rhs_ref, flag_ref, sems):
    whole = pltpu.make_async_copy(k_hbm, held_ref, sems.at[0])
    rhs = pltpu.make_async_copy(rhs_hbm, rhs_ref, sems.at[1])
    flag = pltpu.make_async_copy(flag_hbm, flag_ref, sems.at[2])
    rhs.start()
    flag.start()
    whole.start()
    rhs.wait()
    flag.wait()
    set_face(rhs_ref, flag_ref, 0, g_ref, lo_ref)
    whole.wait()


def first_kernel(par_ref, live_ref, k_ref, own_g_ref, own_lo_ref, prev_ref, flag_prev_ref,
                 near_ref, far_ref, m_ref, q_ref, lo_ref, g_ref, c_ref, u_ref):
    par = par_ref[0, 0]
    live = live_ref[0, 0]
    face = prev_ref.shape[0]
    own = pl.ds(pl.multiple_of(face * par, face), face)
    g_ref[own, :] = own_g_ref[...]
    lo_ref[own, :] = own_lo_ref[...]
    set_face(prev_ref, flag_prev_ref, face * (1 - par), g_ref, lo_ref)
    squares = [jnp.zeros((8, prev_ref.shape[1]), jnp.float32) for _ in range(2)]
    for chunk in range(2 * face // CHUNK):
        rows = pl.ds(chunk * CHUNK, CHUNK)
        half = (chunk * CHUNK) // face
        change = jnp.maximum(-(FIRST_STEP * g_ref[rows, :]), lo_ref[rows, :].astype(jnp.float32))
        m_ref[rows, :] = change
        c_ref[rows, :] = change
        squares[half] = squares[half] + fold(change * change)
        store_operand(par, live, chunk, change, face, u_ref)
    product(par, live, squares, k_ref, u_ref, g_ref, c_ref, q_ref, near_ref, far_ref)


def pair_kernel(near_ref, got_ref, send_ref):
    rows = pl.ds(near_ref.shape[0] - EXTRA, EXTRA)
    both = near_ref[rows, :] + got_ref[rows, :]
    send_ref[...] = jnp.broadcast_to(both[None, 0:2, :], send_ref.shape)


def total_kernel(sums_ref, step_ref):
    total = sums_ref[...]
    count = total.shape[0]
    while count > 1:
        count //= 2
        total = total[:count] + total[count:]
    total = total[0]
    step_ref[...] = (total[0:1, :] + EPSILON) / (total[1:2, :] + EPSILON)


def step_kernel(last, par_ref, live_ref, k_ref, step_ref, near_got, far_got, m_in, q_in, lo_ref, *outs):
    if last:
        top_ref, base_ref, own_ref, u_ref, g_ref, m_ref, c_ref = outs
    else:
        near_ref, far_ref, m_ref, q_ref, g_ref, c_ref, u_ref = outs
    par = par_ref[0, 0]
    live = live_ref[0, 0]
    face = far_got.shape[0]
    step = step_ref[...]
    squares = [jnp.zeros((8, far_got.shape[1]), jnp.float32) for _ in range(2)]
    for chunk in range(2 * face // CHUNK):
        rows = pl.ds(chunk * CHUNK, CHUNK)
        half = (chunk * CHUNK) // face
        inner = pl.ds(chunk * CHUNK - half * face, CHUNK)
        got = (near_got, far_got)[half]
        grad = q_in[rows, :] - sign_of(par, half) * got[inner, :].astype(jnp.float32)
        g_ref[rows, :] = grad
        old = m_in[rows, :]
        moved = jnp.maximum(old - step * grad, lo_ref[rows, :].astype(jnp.float32))
        change = moved - old
        m_ref[rows, :] = moved
        c_ref[rows, :] = change
        if not last:
            squares[half] = squares[half] + fold(change * change)
        store_operand(par, live, chunk, change, face, u_ref)
    if not last:
        product(par, live, squares, k_ref, u_ref, g_ref, c_ref, q_ref, near_ref, far_ref)
        return
    operand = u_ref[...]
    for t in range(face // TILE):
        piece = tile_product(t * TILE, live, k_ref, operand)
        top_ref[pl.ds(t * TILE, TILE), :] = piece.astype(top_ref.dtype)
    own = pl.ds(pl.multiple_of(face * par, face), face)
    own_ref[...] = m_ref[own, :]
    base_ref[...] = g_ref[own, :] + RIDGE * c_ref[own, :]


def tail_kernel(live_ref, k_ref, u_ref, base_ref, own_ref, pre_ref, out_ref):
    face = base_ref.shape[0]
    operand = u_ref[...]
    out_ref[...] = own_ref[...]
    for t in range(face // TILE):
        rows = pl.ds(t * TILE, TILE)
        pre_ref[rows, :] = base_ref[rows, :] + tile_product(face + t * TILE, live_ref[0, 0], k_ref, operand)


def on_device(operators, dual_rhs, contact, costs, *, chips):
    matrix = pltpu.with_memory_space_constraint(operators[0, 0], pltpu.HBM)
    rhs = dual_rhs[0]
    face, cases = rhs.shape
    order = 2 * face
    wide = 2 * chips
    par = lax.axis_index("core").astype(jnp.int32).reshape(1, 1)
    forward = [(i, (i + 1) % wide) for i in range(wide)]
    backward = [((i + 1) % wide, i) for i in range(wide)]
    near_pairs = [(i, i ^ 1) for i in range(wide)]
    far_pairs = [(i, (i + 1) % wide if i % 2 else (i - 1) % wide) for i in range(wide)]

    rhs_prev = lax.ppermute(rhs, WIDE, forward)
    flag_prev = lax.ppermute(contact, WIDE, forward)

    f32, bf16 = jnp.float32, jnp.bfloat16
    send_s = jax.ShapeDtypeStruct((chips, 2, cases), f32)
    near_s = jax.ShapeDtypeStruct((face + EXTRA, cases), f32)
    far_s = jax.ShapeDtypeStruct((face, cases), bf16)
    half_s = jax.ShapeDtypeStruct((face, cases), f32)
    full_s = jax.ShapeDtypeStruct((order, cases), f32)
    low_s = jax.ShapeDtypeStruct((order, cases), bf16)
    full = pltpu.VMEM((order, cases), f32)
    operand = pltpu.VMEM((order, cases), bf16)
    call = functools.partial(
        pl.pallas_call,
        compiler_params=pltpu.CompilerParams(vmem_limit_bytes=16 << 20),
        cost_estimate=pl.CostEstimate(
            flops=2 * order * order * cases, bytes_accessed=2 * order * order, transcendentals=0
        ),
    )

    own_g, own_lo, held = call(
        prep_kernel,
        out_shape=(
            half_s,
            jax.ShapeDtypeStruct((face, cases), bf16),
            jax.ShapeDtypeStruct(matrix.shape, matrix.dtype),
        ),
        in_specs=[HBM] * 3,
        out_specs=(VMEM,) * 3,
        scratch_shapes=[
            pltpu.VMEM(rhs.shape, f32),
            pltpu.VMEM(contact.shape, contact.dtype),
            pltpu.SemaphoreType.DMA((3,)),
        ],
        name="prep",
    )(
        matrix,
        pltpu.with_memory_space_constraint(rhs, pltpu.HBM),
        pltpu.with_memory_space_constraint(contact, pltpu.HBM),
    )
    near, far, m, q, lo = call(
        first_kernel,
        out_shape=(near_s, far_s, full_s, full_s, low_s),
        in_specs=[SMEM, SMEM] + [VMEM] * 5,
        out_specs=(VMEM,) * 5,
        scratch_shapes=[full, full, operand],
        name="first",
    )(par, costs, held, own_g, own_lo, rhs_prev, flag_prev)

    for iteration in range(1, ITERS):
        last = iteration + 1 == ITERS
        near_got = lax.ppermute(near, WIDE, near_pairs)
        far_got = lax.ppermute(far, WIDE, far_pairs)
        send = call(
            pair_kernel,
            out_shape=send_s,
            in_specs=[VMEM, VMEM],
            out_specs=VMEM,
            name="pair",
        )(near, near_got)
        sums = lax.all_to_all(send, "chip", 0, 0)
        steplen = call(
            total_kernel,
            out_shape=jax.ShapeDtypeStruct((1, cases), f32),
            in_specs=[VMEM],
            out_specs=VMEM,
            name="total",
        )(sums)
        args = (par, costs, held, steplen, near_got, far_got, m, q, lo)
        if not last:
            near, far, m, q = call(
                functools.partial(step_kernel, False),
                out_shape=(near_s, far_s, full_s, full_s),
                in_specs=[SMEM, SMEM] + [VMEM] * 7,
                out_specs=(VMEM,) * 4,
                scratch_shapes=[full, full, operand],
                name="step",
            )(*args)
        else:
            top, base, own, u = call(
                functools.partial(step_kernel, True),
                out_shape=(half_s, half_s, half_s, low_s),
                in_specs=[SMEM, SMEM] + [VMEM] * 7,
                out_specs=(VMEM,) * 4,
                scratch_shapes=[full, full, full],
                name="last",
            )(*args)
    got = lax.ppermute(top, WIDE, backward)
    pre, own = call(
        tail_kernel,
        out_shape=(half_s, half_s),
        in_specs=[SMEM] + [VMEM] * 4,
        out_specs=(VMEM,) * 2,
        name="tail",
    )(costs, held, u, base, own)
    gradient = pre - got.astype(f32)
    return own[None], gradient[None]


def solution(mesh):
    chips = mesh.shape["wide"] // 2
    finer = Mesh(mesh.devices.reshape(chips, 2, mesh.shape["lend"]), WIDE + ("lend",))
    return jax.shard_map(
        functools.partial(on_device, chips=chips),
        mesh=finer,
        in_specs=(
            P("lend", WIDE, None, None),
            P("lend", WIDE, None),
            P("lend", WIDE),
            P("lend", WIDE),
        ),
        out_specs=(P("lend", WIDE, None), P("lend", WIDE, None)),
        check_vma=False,
    )
```
